32 devices in a mesh: freq: 2 (over y), row: 4 (over z), col: 4 (over x, core).
Axes of the slice: x: 2, y: 2, z: 4, core: 2. Of those that a mesh axis runs over, the one named last changes fastest.
Arguments:
- traces: bfloat16 [4, 6144, 6144], P('freq', 'row', 'col'), parts along dimension 0, may hold values from -6 to 6
- recv_live: int32 [12288], P('freq'), parts along dimension 0, may hold values 0 or 1
- missing: int32 [8, 96], P('freq'), parts along dimension 0, may hold values from 0 to 1535, as said below
- wavelet: float32 [4], P('freq'), parts along dimension 0, may hold values from 0.5 to 1.5
Outputs:
- primaries: float32 [4, 6144, 512], P('freq', 'row', 'col'), parts along dimension 0
The draws below stay inside these ranges and needn't reach their ends.
There are 2 independent parts, one for each index of `freq`. The reference program is written for one: setup_inputs(seed, part) draws one part's arguments, and reference() takes and returns one part's arrays. A program takes and returns all parts, laid end to end along the dimension named above; each array names one. Nothing has to cross between parts.
Inputs may be any that keep to these rules, and one draw needn't show every extreme that they name: `missing`: each row lists 96 distinct positions within one block of 1536 shots, the shots of that block that were not recorded; the block's first and last shots are always among them.
All inputs are finite; a program needn't handle non-finite values.
Results may differ from the reference program's by a relative error of at most 0.0003.
Values may be sent and summed in bfloat16 or wider, within the bound.
A program may use at most 128 MiB of HBM per device.

```python
import math
import jax
import jax.numpy as jnp
from jax import lax

ORDER = 6144
WIN = 128
MISS = 96
TILE = 1536
BLOCKS = 4
N_ROW = 4


def draw_missing(key, part):
    sub_keys = jax.random.split(key, BLOCKS)

    def one_block(sub_key):
        shuffled = jax.random.permutation(sub_key, TILE - 2)[:MISS - 2] + 1
        ends = jnp.array([0, TILE - 1], jnp.int32)
        return jnp.concatenate([ends, shuffled.astype(jnp.int32)])
    return jax.vmap(one_block)(sub_keys)


def set_ends(drawn, key, least, top_value):
    shape = drawn.shape
    index_at = [jax.random.randint(jax.random.fold_in(key, axis), (), 0, shape[axis]) for axis in range(len(shape))]
    drawn = drawn.at[tuple(index_at)].set(least)
    longest = shape.index(max(shape))
    index_at[longest] = (index_at[longest] + 1) % shape[longest]
    return drawn.at[tuple(index_at)].set(top_value)


def block_scale(key, shape, pieces, smallest, high):
    def one(position, blocks):
        heights = jax.random.uniform(jax.random.fold_in(jax.random.fold_in(key, 6), position), (blocks,), jnp.float32, smallest / len(pieces), high / len(pieces))
        return jnp.repeat(jnp.exp(heights), shape[position] // blocks).reshape((-1,) + (1,) * (len(shape) - position - 1))

    loudness = one(*pieces[0])
    for cut in pieces[1:]:
        loudness = loudness * one(*cut)
    return loudness


def centred(rng, shape, spread, limit, shards=(), held_as=jnp.bfloat16):
    gain = block_scale(rng, shape, shards, -0.22, 0.18) if shards else 1.0
    values = jax.random.normal(rng, shape, jnp.float32) * spread * gain
    return jnp.minimum(jnp.maximum(values, -limit), limit).astype(held_as)


def setup_inputs(seed: int = 0, part: int = 0) -> dict:
    arg_keys = jax.random.split(jax.random.key(seed), 5)
    part_keys = jax.random.split(jax.random.fold_in(arg_keys[4], part), 5)
    return {
        "traces": centred(part_keys[0], (2, ORDER, ORDER), 1.0, 6.0, ((1, 4), (2, 4))),
        "recv_live": set_ends((jax.random.randint(part_keys[1], (ORDER,), 0, 8) < 7).astype(jnp.int32), jax.random.fold_in(part_keys[1], 1), 0, 1),
        "missing": draw_missing(jax.random.fold_in(jax.random.fold_in(arg_keys[4], part), 71), part),
        "wavelet": jnp.clip(jax.random.uniform(part_keys[3], (2,), jnp.float32, 0.5, 1.5), 0.5, 1.5),
    }


def reference(traces, recv_live, missing, wavelet):
    tile_size = ORDER // N_ROW
    positions = jnp.arange(tile_size, dtype=jnp.int32)
    dead_rows = jnp.any(positions[None, :, None] == missing[:, None, :], axis=2).reshape(ORDER)
    shot_live = jnp.logical_not(dead_rows)
    recv_mask = recv_live == 1
    zero_bf = jnp.zeros((), jnp.bfloat16)
    direct = jnp.where(recv_mask[None, None, :], traces, zero_bf)
    flipped = jnp.swapaxes(traces, 1, 2)
    mirrored = jnp.where(recv_mask[None, :, None] & shot_live[None, None, :], flipped, zero_bf)
    filled = jnp.where(shot_live[None, :, None], direct, mirrored).astype(jnp.bfloat16)
    window = filled.reshape(2, ORDER, N_ROW, tile_size)[:, :, :, :WIN].reshape(2, ORDER, N_ROW * WIN)
    left_tile = filled.astype(jnp.float32)
    right_tile = window.astype(jnp.float32)

    def matmul(first, second):
        return jnp.dot(first, second, precision=lax.Precision.HIGHEST, preferred_element_type=jnp.float32)
    real_part = matmul(left_tile[0], right_tile[0]) - matmul(left_tile[1], right_tile[1])
    imag_part = matmul(left_tile[0], right_tile[1]) + matmul(left_tile[1], right_tile[0])
    norm_scale = 1.0 / math.sqrt(ORDER)
    pred_real = (wavelet[0] * real_part - wavelet[1] * imag_part) * norm_scale
    pred_imag = (wavelet[0] * imag_part + wavelet[1] * real_part) * norm_scale
    return jnp.stack([right_tile[0] - pred_real, right_tile[1] - pred_imag])
```

```python
import math

import jax
import jax.numpy as jnp
from jax import lax
from jax.sharding import PartitionSpec as P

F32 = jnp.float32
BF16 = jnp.bfloat16


def dot(first, second, dims=((1,), (0,)), **kw):
    return lax.dot_general(first, second, (dims, ((), ())), preferred_element_type=F32, **kw)


def make_local(order):
    def local(traces, recv_live, missing, wavelet):
        tile = traces.shape[1]
        grid = lax.axis_size("row")
        win = 128
        row = lax.axis_index("row")
        col = lax.axis_index("col")
        positions = jnp.arange(tile, dtype=jnp.int32)
        raw = traces[:, :, :win]
        gathered = lax.all_gather(raw, "row", axis=0, tiled=False)

        miss_row = lax.dynamic_index_in_dim(missing, row, 0, keepdims=False)
        miss_col = lax.dynamic_index_in_dim(missing, col, 0, keepdims=False)
        hot_row = positions[None, :] == miss_row[:, None]
        hot_col = positions[None, :] == miss_col[:, None]
        dead_row = jnp.any(hot_row, axis=0)
        dead_col = jnp.any(hot_col, axis=0)
        dead_win = jnp.any(missing[:, :, None] == positions[None, None, :win], axis=1)
        recv = (recv_live == 1).reshape(grid, tile)
        recv_row = lax.dynamic_index_in_dim(recv, row, 0, keepdims=False)
        recv_col = lax.dynamic_index_in_dim(recv, col, 0, keepdims=False)
        recv_miss_row = jnp.any(hot_row & recv_row[None, :], axis=1)
        recv_miss_col = jnp.any(hot_col & recv_col[None, :], axis=1)
        hot_row_b = hot_row.astype(BF16)
        hot_col_b = hot_col.astype(BF16)
        zero = jnp.zeros((), BF16)

        outgoing = jnp.stack([dot(hot_col_b, traces[p], ((1,), (1,))) for p in range(2)]).astype(BF16)
        route = [(r * grid + c, c * grid + r) for r in range(grid) for c in range(grid)]
        incoming = lax.ppermute(outgoing, ("row", "col"), route)
        dead_gather = lax.all_gather(outgoing[:, :, :win], "row", axis=0, tiled=False)

        swapped = lax.all_to_all(gathered, "col", split_axis=0, concat_axis=0, tiled=True)
        wide = jnp.transpose(swapped, (1, 2, 0, 3)).reshape(2, tile, grid * win)
        live_win = recv[:, :win].reshape(-1)
        keep = jnp.where(live_win[None, :] & ~dead_col[:, None], True, False)
        deads = jnp.transpose(dead_gather, (1, 2, 0, 3)).reshape(2, -1, grid * win)
        dead_keep = recv_miss_col[:, None] & ~dead_win.reshape(-1)[None, :]
        deads = jnp.where(dead_keep[None], deads, zero)
        window = [
            jnp.where(keep, wide[p], dot(hot_col_b, deads[p], ((0,), (0,))).astype(BF16))
            for p in range(2)
        ]
        masked = [jnp.where(recv_col[:, None], w, zero) for w in window]
        patched = jnp.where(recv_miss_row[None, :, None] & ~dead_col[None, None, :], incoming, zero)

        def product(left, right):
            first = jnp.concatenate([right[0], right[1]], axis=1)
            second = jnp.concatenate([-right[1], right[0]], axis=1)
            return dot(left[0], first) + dot(left[1], second)

        live = product(traces, masked)
        lost = product(patched, window)
        lost = dot(hot_row.astype(F32), lost, ((0,), (0,)), precision=lax.Precision.HIGHEST)
        partial = jnp.where(dead_row[:, None], lost, live)
        partial = jnp.transpose(partial.reshape(tile, 2, grid, win), (2, 1, 0, 3))
        total = lax.psum_scatter(partial, "col", scatter_dimension=0, tiled=True)[0]
        scale = 1.0 / math.sqrt(order)
        real = (wavelet[0] * total[0] - wavelet[1] * total[1]) * scale
        imag = (wavelet[0] * total[1] + wavelet[1] * total[0]) * scale
        own_in = lax.dynamic_index_in_dim(recv[:, :win], col, 0, keepdims=False)
        own_dead = jnp.where(
            recv_miss_row[None, :, None] & ~dead_col[None, None, :win], incoming[:, :, :win], zero
        )
        own = [
            jnp.where(
                dead_row[:, None],
                dot(hot_row_b, own_dead[p], ((0,), (0,))),
                jnp.where(own_in[None, :], raw[p], zero).astype(F32),
            )
            for p in range(2)
        ]
        return jnp.stack([own[0] - real, own[1] - imag])

    return local


def solution(mesh):
    in_specs = (P("freq", "row", "col"), P("freq"), P("freq", None), P("freq"))
    out_specs = P("freq", "row", "col")

    def run(traces, recv_live, missing, wavelet):
        local = make_local(traces.shape[1])
        return jax.shard_map(
            local, mesh=mesh, in_specs=in_specs, out_specs=out_specs, check_vma=False
        )(traces, recv_live, missing, wavelet)

    return run
```

```python
import functools
import math

import jax
import jax.numpy as jnp
from jax import lax
from jax.experimental import pallas as pl
from jax.experimental.pallas import tpu as pltpu
from jax.sharding import PartitionSpec as P

F32 = jnp.float32
BF16 = jnp.bfloat16
CHUNKS = 3
MESH = pl.DeviceIdType.MESH


def dot(first, second, dims=((1,), (0,))):
    return lax.dot_general(first, second, (dims, ((), ())), preferred_element_type=F32)


def kernel(
    grid, scale, wav, traces, hot_col, hot_col_t, hot_row_t, patch_keep, recv_lane, live_row,
    live_col, win_live, dead_keep, out,
    full, gath, wbuf, mir_out, mir_in, deads, wide, part_out, part_in,
    full_sem, own_sem, right_sem, left_sem, z_sem, across_sem, w_sem, mir_sem, dead_send, dead_recv,
    part_send, part_recv,
):
    row = lax.axis_index("row")
    col = lax.axis_index("col")
    tile = traces.shape[1]
    win = out.shape[2]
    chunk = tile // CHUNKS
    far = jnp.where(row > col, row - col, col - row)

    def remote(src, dst, send, recv, to_row, to_col):
        return pltpu.make_async_remote_copy(
            src_ref=src, dst_ref=dst, send_sem=send, recv_sem=recv,
            device_id={"row": to_row, "col": to_col}, device_id_type=MESH,
        )

    def right(c, p):
        return remote(gath.at[c, p], gath.at[c, p], right_sem.at[c, p], z_sem.at[c, p], row + 1, col)

    def left(c, p):
        return remote(gath.at[c, p], gath.at[c, p], left_sem.at[c, p], z_sem.at[c, p], row - 1, col)

    def across(c, b, p):
        return remote(gath.at[c, p], wbuf.at[b, p], across_sem.at[c, p], w_sem.at[b, p], row, c)

    def mirror():
        return remote(mir_out, mir_in, mir_sem.at[0], mir_sem.at[1], col, row)

    def dead(target, source):
        return remote(
            mir_out.at[:, :, pl.ds(0, win)], deads.at[source], dead_send.at[target],
            dead_recv.at[source], target, col,
        )

    def partial(b, source, k):
        span = pl.ds(k * chunk, chunk)
        return remote(
            part_out.at[b, :, span], part_in.at[source, :, span], part_send.at[b, k],
            part_recv.at[source, k], row, b,
        )

    owns = [
        pltpu.make_async_copy(traces.at[p, :, pl.ds(0, win)], gath.at[row, p], own_sem.at[p])
        for p in range(2)
    ]
    loads = [pltpu.make_async_copy(traces.at[p], full.at[p], full_sem.at[p]) for p in range(2)]
    for copy in owns + loads:
        copy.start()

    barrier = pltpu.get_barrier_semaphore()

    def greet(i, _):
        @pl.when(i != col)
        def _():
            pl.semaphore_signal(barrier, inc=1, device_id={"row": row, "col": i}, device_id_type=MESH)

        @pl.when(i != row)
        def _():
            pl.semaphore_signal(barrier, inc=1, device_id={"row": i, "col": col}, device_id_type=MESH)

        return 0

    lax.fori_loop(0, grid, greet, 0)

    @pl.when(row != col)
    def _():
        pl.semaphore_signal(barrier, inc=1, device_id={"row": col, "col": row}, device_id_type=MESH)
        pl.semaphore_wait(barrier, 2 * grid - 1)

    @pl.when(row == col)
    def _():
        pl.semaphore_wait(barrier, 2 * grid - 2)

    def pass_on(c, p, go_right, go_left):
        if go_right:
            @pl.when(row + 1 < grid)
            def _():
                right(c, p).start()

        if go_left:
            @pl.when(row > 0)
            def _():
                left(c, p).start()

        @pl.when(c != col)
        def _():
            across(c, col, p).start()

    for p in range(2):
        owns[p].wait()
        pass_on(row, p, True, True)

    for p in range(2):
        loads[p].wait()
        mir_out[p] = dot(hot_col[...], full[p], ((1,), (1,))).astype(BF16)

    @pl.when(row != col)
    def _():
        mirror().start()

    def send_dead(i, _):
        @pl.when(i != row)
        def _():
            dead(i, row).start()

        return 0

    lax.fori_loop(0, grid, send_dead, 0)

    def build_full():
        @pl.when(row != col)
        def _():
            mirror().wait_recv()
            mir_in[...] = mir_in[...] * patch_keep[...][None]

        @pl.when(row == col)
        def _():
            mir_in[...] = mir_out[...] * patch_keep[...][None]

        def some(k, _):
            span = pl.ds(pl.multiple_of(k * 128, 128), 128)
            for p in range(2):
                kept = full[p, span, :].astype(F32) * recv_lane[...] * live_row[span, :]
                full[p, span, :] = (kept + dot(hot_row_t[span, :], mir_in[p])).astype(BF16)
            return 0

        lax.fori_loop(0, tile // 128, some, 0)

    def widen(source, b, lost):
        for p in range(2):
            raw = source[p].astype(F32) * win_live[b] * live_col[...]
            extra = dot(hot_col_t[...], lost[p] * dead_keep[b])
            value = (raw + extra).astype(BF16)
            if p == 0:
                wide[0, :, :win] = value
                wide[1, :, win:] = value
            else:
                wide[0, :, win:] = value
                wide[1, :, :win] = -value

    def multiply():
        def block(t, _):
            chip = lax.rem(col // 2 + grid // 2 - 1 - t // 2, grid // 2)
            b = 2 * chip + lax.rem(col + 1 + t, 2)

            @pl.when(b != row)
            def _():
                dead(b, b).wait_recv()

            @pl.when(b == row)
            def _():
                deads[row] = mir_out[:, :, :win]

            @pl.when(b != col)
            def _():
                for p in range(2):
                    across(col, b, p).wait_recv()
                widen(wbuf.at[b], b, deads.at[b])

            @pl.when(b == col)
            def _():
                widen(gath.at[col], b, deads.at[b])

            def rows(k, _):
                span = pl.ds(pl.multiple_of(k * chunk, chunk), chunk)
                both = dot(full[0, span, :], wide[0]) + dot(full[1, span, :], wide[1])
                part_out[b, 0, span, :] = both[:, :win]
                part_out[b, 1, span, :] = both[:, win:]

                @pl.when(b != col)
                def _():
                    partial(b, col, k).start()

                return 0

            lax.fori_loop(0, CHUNKS, rows, 0)
            return 0

        lax.fori_loop(0, grid, block, 0)

    @pl.when(far == 0)
    def _():
        build_full()

    def step(s, _):
        @pl.when(s > 0)
        def _():
            for p in range(2):
                @pl.when(row - s >= 0)
                def _():
                    left(row - s, p).wait_recv()
                    pass_on(row - s, p, True, False)

                @pl.when(row + s < grid)
                def _():
                    right(row + s, p).wait_recv()
                    pass_on(row + s, p, False, True)

        @pl.when((s == 1) & (far > 0))
        def _():
            build_full()

        @pl.when(s == far)
        def _():
            multiply()

        return 0

    lax.fori_loop(0, grid, step, 0)

    def arrive(i, _):
        @pl.when(i != col)
        def _():
            for k in range(CHUNKS):
                partial(i, i, k).wait_recv()

        @pl.when(i == col)
        def _():
            part_in[col] = part_out[col]

        return 0

    lax.fori_loop(0, grid, arrive, 0)
    first, second = wav[0] * scale, wav[1] * scale

    def finish(k, _):
        span = pl.ds(pl.multiple_of(k * 128, 128), 128)
        real = part_in[0, 0, span, :]
        imag = part_in[0, 1, span, :]
        for i in range(1, grid):
            real = real + part_in[i, 0, span, :]
            imag = imag + part_in[i, 1, span, :]
        out[0, span, :] = full[0, span, :win].astype(F32) - (first * real - second * imag)
        out[1, span, :] = full[1, span, :win].astype(F32) - (first * imag + second * real)
        return 0

    lax.fori_loop(0, tile // 128, finish, 0)

    def drain(i, _):
        for p in range(2):
            @pl.when((row + 1 < grid) & (i <= row))
            def _():
                right(i, p).wait_send()

            @pl.when((row > 0) & (i >= row))
            def _():
                left(i, p).wait_send()

            @pl.when(i != col)
            def _():
                across(i, col, p).wait_send()

        @pl.when(i != row)
        def _():
            dead(i, row).wait_send()

        @pl.when(i != col)
        def _():
            for k in range(CHUNKS):
                partial(i, col, k).wait_send()

        return 0

    lax.fori_loop(0, grid, drain, 0)

    @pl.when(row != col)
    def _():
        mirror().wait_send()


def make_local(order):
    def local(traces, recv_live, missing, wavelet):
        tile = traces.shape[1]
        grid = lax.axis_size("row")
        lost = missing.shape[1]
        win = 128
        row = lax.axis_index("row")
        col = lax.axis_index("col")
        positions = jnp.arange(tile, dtype=jnp.int32)
        miss_row = lax.dynamic_index_in_dim(missing, row, 0, keepdims=False)
        miss_col = lax.dynamic_index_in_dim(missing, col, 0, keepdims=False)
        hot_row = positions[None, :] == miss_row[:, None]
        hot_col = positions[None, :] == miss_col[:, None]
        live_row = ~jnp.any(hot_row, axis=0)
        live_col = ~jnp.any(hot_col, axis=0)
        dead_win = jnp.any(missing[:, :, None] == positions[None, None, :win], axis=1)
        recv = (recv_live == 1).reshape(grid, tile)
        recv_row = lax.dynamic_index_in_dim(recv, row, 0, keepdims=False)
        recv_col = lax.dynamic_index_in_dim(recv, col, 0, keepdims=False)
        recv_miss_row = jnp.any(hot_row & recv_row[None, :], axis=1)
        recv_miss_col = jnp.any(hot_col & recv_col[None, :], axis=1)
        operands = (
            wavelet,
            traces,
            hot_col.astype(BF16),
            (positions[:, None] == miss_col[None, :]).astype(BF16),
            (positions[:, None] == miss_row[None, :]).astype(BF16),
            (recv_miss_row[:, None] & live_col[None, :]).astype(BF16),
            recv_col[None, :].astype(F32),
            live_row[:, None].astype(F32),
            live_col[:, None].astype(F32),
            recv[:, None, :win].astype(F32),
            (recv_miss_col[None, :, None] & ~dead_win[:, None, :]).astype(BF16),
        )
        vmem = pl.BlockSpec(memory_space=pltpu.VMEM)
        dma = pltpu.SemaphoreType.DMA
        return pl.pallas_call(
            functools.partial(kernel, grid, 1.0 / math.sqrt(order)),
            out_shape=jax.ShapeDtypeStruct((2, tile, win), F32),
            in_specs=[pl.BlockSpec(memory_space=pltpu.SMEM), pl.BlockSpec(memory_space=pl.ANY)]
            + [vmem] * 9,
            out_specs=vmem,
            scratch_shapes=[
                pltpu.VMEM((2, tile, tile), BF16),
                pltpu.VMEM((grid, 2, tile, win), BF16),
                pltpu.VMEM((grid, 2, tile, win), BF16),
                pltpu.VMEM((2, lost, tile), BF16),
                pltpu.VMEM((2, lost, tile), BF16),
                pltpu.VMEM((grid, 2, lost, win), BF16),
                pltpu.VMEM((2, tile, 2 * win), BF16),
                pltpu.VMEM((grid, 2, tile, win), F32),
                pltpu.VMEM((grid, 2, tile, win), F32),
                dma((2,)), dma((2,)), dma((grid, 2)), dma((grid, 2)), dma((grid, 2)),
                dma((grid, 2)), dma((grid, 2)), dma((2,)), dma((grid,)), dma((grid,)),
                dma((grid, CHUNKS)), dma((grid, CHUNKS)),
            ],
            compiler_params=pltpu.CompilerParams(
                collective_id=0, has_side_effects=True, vmem_limit_bytes=60 * 1024 * 1024
            ),
            name="predict",
        )(*operands)

    return local


def solution(mesh):
    in_specs = (P("freq", "row", "col"), P("freq"), P("freq", None), P("freq"))
    out_specs = P("freq", "row", "col")

    def run(traces, recv_live, missing, wavelet):
        local = make_local(traces.shape[1])
        return jax.shard_map(
            local, mesh=mesh, in_specs=in_specs, out_specs=out_specs, check_vma=False
        )(traces, recv_live, missing, wavelet)

    return run
```

```python
import functools
import math

import jax
import jax.numpy as jnp
from jax import lax
from jax.experimental import pallas as pl
from jax.experimental.pallas import tpu as pltpu
from jax.sharding import PartitionSpec as P

F32 = jnp.float32
BF16 = jnp.bfloat16
CHUNKS = 3
MESH = pl.DeviceIdType.MESH


def dot(first, second, dims=((1,), (0,))):
    return lax.dot_general(first, second, (dims, ((), ())), preferred_element_type=F32)


def kernel(
    grid, scale, wav, traces, hot_col, hot_col_t, hot_row_t, patch_keep, recv_lane, live_row,
    live_col, win_live, dead_keep, out,
    full, gath, wbuf, mir_out, mir_in, deads, wide, part_out, pair_in, chip_in,
    full_sem, own_sem, right_sem, left_sem, z_sem, across_sem, w_sem, mir_sem, dead_send, dead_recv,
    pair_send, pair_recv, chip_send, chip_recv,
):
    row = lax.axis_index("row")
    col = lax.axis_index("col")
    tile = traces.shape[1]
    win = out.shape[2]
    chunk = tile // CHUNKS
    chips = grid // 2
    home = col // 2
    side = lax.rem(col, 2)
    mate = 2 * home + 1 - side
    far = jnp.where(row > col, row - col, col - row)
    far_mate = jnp.where(row > mate, row - mate, mate - row)
    turn = jnp.minimum(far + 1, grid - 1)
    turn_mate = jnp.minimum(far_mate + 1, grid - 1)

    def remote(src, dst, send, recv, to_row, to_col):
        return pltpu.make_async_remote_copy(
            src_ref=src, dst_ref=dst, send_sem=send, recv_sem=recv,
            device_id={"row": to_row, "col": to_col}, device_id_type=MESH,
        )

    def right(c, p):
        return remote(gath.at[c, p], gath.at[c, p], right_sem.at[c, p], z_sem.at[c, p], row + 1, col)

    def left(c, p):
        return remote(gath.at[c, p], gath.at[c, p], left_sem.at[c, p], z_sem.at[c, p], row - 1, col)

    def across(c, b, p):
        return remote(gath.at[c, p], wbuf.at[b, p], across_sem.at[c, p], w_sem.at[b, p], row, c)

    def mirror():
        return remote(mir_out, mir_in, mir_sem.at[0], mir_sem.at[1], col, row)

    def dead(target, source):
        return remote(
            mir_out.at[:, :, pl.ds(0, win)], deads.at[source], dead_send.at[target],
            dead_recv.at[source], target, col,
        )

    def pair(chip, k):
        span = pl.ds(k * chunk, chunk)
        return remote(
            part_out.at[2 * chip + 1 - side, :, span], pair_in.at[chip, :, span],
            pair_send.at[chip, k], pair_recv.at[chip, k], row, mate,
        )

    def cross(chip, source, k):
        span = pl.ds(k * chunk, chunk)
        return remote(
            part_out.at[2 * chip + side, :, span], chip_in.at[source, :, span],
            chip_send.at[chip, k], chip_recv.at[source, k], row, 2 * chip + side,
        )

    def merge(chip, k):
        pair(chip, k).wait_recv()
        b = 2 * chip + side
        span = pl.ds(pl.multiple_of(k * chunk, chunk), chunk)
        part_out[b, :, span, :] = part_out[b, :, span, :] + pair_in[chip, :, span, :]
        cross(chip, home, k).start()

    owns = [
        pltpu.make_async_copy(traces.at[p, :, pl.ds(0, win)], gath.at[row, p], own_sem.at[p])
        for p in range(2)
    ]
    loads = [pltpu.make_async_copy(traces.at[p], full.at[p], full_sem.at[p]) for p in range(2)]
    for copy in owns + loads:
        copy.start()

    barrier = pltpu.get_barrier_semaphore()

    def greet(i, _):
        @pl.when(i != col)
        def _():
            pl.semaphore_signal(barrier, inc=1, device_id={"row": row, "col": i}, device_id_type=MESH)

        @pl.when(i != row)
        def _():
            pl.semaphore_signal(barrier, inc=1, device_id={"row": i, "col": col}, device_id_type=MESH)

        return 0

    lax.fori_loop(0, grid, greet, 0)

    @pl.when(row != col)
    def _():
        pl.semaphore_signal(barrier, inc=1, device_id={"row": col, "col": row}, device_id_type=MESH)
        pl.semaphore_wait(barrier, 2 * grid - 1)

    @pl.when(row == col)
    def _():
        pl.semaphore_wait(barrier, 2 * grid - 2)

    def pass_on(c, p, go_right, go_left):
        if go_right:
            @pl.when(row + 1 < grid)
            def _():
                right(c, p).start()

        if go_left:
            @pl.when(row > 0)
            def _():
                left(c, p).start()

        @pl.when(c != col)
        def _():
            across(c, col, p).start()

    for p in range(2):
        owns[p].wait()
        pass_on(row, p, True, True)

    for p in range(2):
        loads[p].wait()
        mir_out[p] = dot(hot_col[...], full[p], ((1,), (1,))).astype(BF16)

    @pl.when(row != col)
    def _():
        mirror().start()

    def send_dead(i, _):
        @pl.when(i != row)
        def _():
            dead(i, row).start()

        return 0

    lax.fori_loop(0, grid, send_dead, 0)

    def build_full():
        @pl.when(row != col)
        def _():
            mirror().wait_recv()
            mir_in[...] = mir_in[...] * patch_keep[...][None]

        @pl.when(row == col)
        def _():
            mir_in[...] = mir_out[...] * patch_keep[...][None]

        def some(k, _):
            span = pl.ds(pl.multiple_of(k * 128, 128), 128)
            for p in range(2):
                kept = full[p, span, :].astype(F32) * recv_lane[...] * live_row[span, :]
                full[p, span, :] = (kept + dot(hot_row_t[span, :], mir_in[p])).astype(BF16)
            return 0

        lax.fori_loop(0, tile // 128, some, 0)

    def widen(source, b, lost):
        for p in range(2):
            raw = source[p].astype(F32) * win_live[b] * live_col[...]
            extra = dot(hot_col_t[...], lost[p] * dead_keep[b])
            value = (raw + extra).astype(BF16)
            if p == 0:
                wide[0, :, :win] = value
                wide[1, :, win:] = value
            else:
                wide[0, :, win:] = value
                wide[1, :, :win] = -value

    def multiply():
        def block(t, _):
            chip = lax.rem(home + chips - 1 - t // 2, chips)
            mine = lax.rem(t, 2)
            b = 2 * chip + lax.rem(col + 1 + t, 2)

            @pl.when(b != row)
            def _():
                dead(b, b).wait_recv()

            @pl.when(b == row)
            def _():
                deads[row] = mir_out[:, :, :win]

            @pl.when(b != col)
            def _():
                for p in range(2):
                    across(col, b, p).wait_recv()
                widen(wbuf.at[b], b, deads.at[b])

            @pl.when(b == col)
            def _():
                widen(gath.at[col], b, deads.at[b])

            def rows(k, _):
                span = pl.ds(pl.multiple_of(k * chunk, chunk), chunk)
                both = dot(full[0, span, :], wide[0]) + dot(full[1, span, :], wide[1])
                part_out[b, 0, span, :] = both[:, :win]
                part_out[b, 1, span, :] = both[:, win:]

                @pl.when(mine == 0)
                def _():
                    pair(chip, k).start()

                @pl.when((mine == 1) & (chip != home) & (far > far_mate))
                def _():
                    merge(chip, k)

                return 0

            lax.fori_loop(0, CHUNKS, rows, 0)
            return 0

        lax.fori_loop(0, grid, block, 0)

    @pl.when(far == 0)
    def _():
        build_full()

    def step(s, _):
        @pl.when(s > 0)
        def _():
            for p in range(2):
                @pl.when(row - s >= 0)
                def _():
                    left(row - s, p).wait_recv()
                    pass_on(row - s, p, True, False)

                @pl.when(row + s < grid)
                def _():
                    right(row + s, p).wait_recv()
                    pass_on(row + s, p, False, True)

        @pl.when((s == min(2, grid - 1)) & (far > 0))
        def _():
            build_full()

        @pl.when(s == turn)
        def _():
            multiply()

        @pl.when((s == turn_mate) & (far < far_mate))
        def _():
            def some(i, _):
                for k in range(CHUNKS):
                    merge(lax.rem(home + 1 + i, chips), k)
                return 0

            lax.fori_loop(0, chips - 1, some, 0)

        return 0

    lax.fori_loop(0, grid, step, 0)

    def arrive(i, _):
        for k in range(CHUNKS):
            @pl.when(i != home)
            def _():
                cross(i, i, k).wait_recv()

            @pl.when(i == home)
            def _():
                pair(home, k).wait_recv()

        return 0

    lax.fori_loop(0, chips, arrive, 0)
    first, second = wav[0] * scale, wav[1] * scale

    def finish(k, _):
        span = pl.ds(pl.multiple_of(k * 128, 128), 128)
        real = part_out[col, 0, span, :] + pair_in[home, 0, span, :]
        imag = part_out[col, 1, span, :] + pair_in[home, 1, span, :]
        for i in range(1, chips):
            other = lax.rem(home + i, chips)
            real = real + chip_in[other, 0, span, :]
            imag = imag + chip_in[other, 1, span, :]
        out[0, span, :] = full[0, span, :win].astype(F32) - (first * real - second * imag)
        out[1, span, :] = full[1, span, :win].astype(F32) - (first * imag + second * real)
        return 0

    lax.fori_loop(0, tile // 128, finish, 0)

    def drain(i, _):
        for p in range(2):
            @pl.when((row + 1 < grid) & (i <= row))
            def _():
                right(i, p).wait_send()

            @pl.when((row > 0) & (i >= row))
            def _():
                left(i, p).wait_send()

            @pl.when(i != col)
            def _():
                across(i, col, p).wait_send()

        @pl.when(i != row)
        def _():
            dead(i, row).wait_send()

        return 0

    lax.fori_loop(0, grid, drain, 0)

    def drain_sums(i, _):
        for k in range(CHUNKS):
            pair(i, k).wait_send()

            @pl.when(i != home)
            def _():
                cross(i, home, k).wait_send()

        return 0

    lax.fori_loop(0, chips, drain_sums, 0)

    @pl.when(row != col)
    def _():
        mirror().wait_send()


def make_local(order):
    def local(traces, recv_live, missing, wavelet):
        tile = traces.shape[1]
        grid = lax.axis_size("row")
        lost = missing.shape[1]
        win = 128
        row = lax.axis_index("row")
        col = lax.axis_index("col")
        positions = jnp.arange(tile, dtype=jnp.int32)
        miss_row = lax.dynamic_index_in_dim(missing, row, 0, keepdims=False)
        miss_col = lax.dynamic_index_in_dim(missing, col, 0, keepdims=False)
        hot_row = positions[None, :] == miss_row[:, None]
        hot_col = positions[None, :] == miss_col[:, None]
        live_row = ~jnp.any(hot_row, axis=0)
        live_col = ~jnp.any(hot_col, axis=0)
        dead_win = jnp.any(missing[:, :, None] == positions[None, None, :win], axis=1)
        recv = (recv_live == 1).reshape(grid, tile)
        recv_row = lax.dynamic_index_in_dim(recv, row, 0, keepdims=False)
        recv_col = lax.dynamic_index_in_dim(recv, col, 0, keepdims=False)
        recv_miss_row = jnp.any(hot_row & recv_row[None, :], axis=1)
        recv_miss_col = jnp.any(hot_col & recv_col[None, :], axis=1)
        operands = (
            wavelet,
            traces,
            hot_col.astype(BF16),
            (positions[:, None] == miss_col[None, :]).astype(BF16),
            (positions[:, None] == miss_row[None, :]).astype(BF16),
            (recv_miss_row[:, None] & live_col[None, :]).astype(BF16),
            recv_col[None, :].astype(F32),
            live_row[:, None].astype(F32),
            live_col[:, None].astype(F32),
            recv[:, None, :win].astype(F32),
            (recv_miss_col[None, :, None] & ~dead_win[:, None, :]).astype(BF16),
        )
        vmem = pl.BlockSpec(memory_space=pltpu.VMEM)
        dma = pltpu.SemaphoreType.DMA
        return pl.pallas_call(
            functools.partial(kernel, grid, 1.0 / math.sqrt(order)),
            out_shape=jax.ShapeDtypeStruct((2, tile, win), F32),
            in_specs=[pl.BlockSpec(memory_space=pltpu.SMEM), pl.BlockSpec(memory_space=pl.ANY)]
            + [vmem] * 9,
            out_specs=vmem,
            scratch_shapes=[
                pltpu.VMEM((2, tile, tile), BF16),
                pltpu.VMEM((grid, 2, tile, win), BF16),
                pltpu.VMEM((grid, 2, tile, win), BF16),
                pltpu.VMEM((2, lost, tile), BF16),
                pltpu.VMEM((2, lost, tile), BF16),
                pltpu.VMEM((grid, 2, lost, win), BF16),
                pltpu.VMEM((2, tile, 2 * win), BF16),
                pltpu.VMEM((grid, 2, tile, win), F32),
                pltpu.VMEM((grid // 2, 2, tile, win), F32),
                pltpu.VMEM((grid // 2, 2, tile, win), F32),
                dma((2,)), dma((2,)), dma((grid, 2)), dma((grid, 2)), dma((grid, 2)),
                dma((grid, 2)), dma((grid, 2)), dma((2,)), dma((grid,)), dma((grid,)),
                dma((grid // 2, CHUNKS)), dma((grid // 2, CHUNKS)),
                dma((grid // 2, CHUNKS)), dma((grid // 2, CHUNKS)),
            ],
            compiler_params=pltpu.CompilerParams(
                collective_id=0, has_side_effects=True, vmem_limit_bytes=60 * 1024 * 1024
            ),
            name="predict",
        )(*operands)

    return local


def solution(mesh):
    in_specs = (P("freq", "row", "col"), P("freq"), P("freq", None), P("freq"))
    out_specs = P("freq", "row", "col")

    def run(traces, recv_live, missing, wavelet):
        local = make_local(traces.shape[1])
        return jax.shard_map(
            local, mesh=mesh, in_specs=in_specs, out_specs=out_specs, check_vma=False
        )(traces, recv_live, missing, wavelet)

    return run
```

```python
import functools
import math

import jax
import jax.numpy as jnp
from jax import lax
from jax.experimental import pallas as pl
from jax.experimental.pallas import tpu as pltpu
from jax.sharding import PartitionSpec as P

F32 = jnp.float32
BF16 = jnp.bfloat16
CHUNKS = 3
MESH = pl.DeviceIdType.MESH


def dot(first, second, dims=((1,), (0,))):
    return lax.dot_general(first, second, (dims, ((), ())), preferred_element_type=F32)


def kernel(
    grid, scale, wav, traces, hot_col, hot_col_t, hot_row_t, patch_keep, recv_lane, live_row,
    live_col, win_live, dead_keep, out,
    full, gath, wbuf, mir_out, mir_in, deads, wide, part_out, pair_in, chip_in,
    full_sem, own_sem, right_sem, left_sem, z_sem, across_sem, w_sem, mir_sem, dead_send, dead_recv,
    pair_send, pair_recv, chip_send, chip_recv,
):
    row = lax.axis_index("row")
    col = lax.axis_index("col")
    tile = traces.shape[1]
    win = out.shape[2]
    chunk = tile // CHUNKS
    chips = grid // 2
    home = col // 2
    side = lax.rem(col, 2)
    mate = 2 * home + 1 - side
    far = jnp.where(row > col, row - col, col - row)
    far_mate = jnp.where(row > mate, row - mate, mate - row)
    last = jnp.maximum(row, grid - 1 - row)
    turn = jnp.minimum(far + 1, last)
    inline = (far > far_mate) & (turn == last)

    def remote(src, dst, send, recv, to_row, to_col):
        return pltpu.make_async_remote_copy(
            src_ref=src, dst_ref=dst, send_sem=send, recv_sem=recv,
            device_id={"row": to_row, "col": to_col}, device_id_type=MESH,
        )

    def right(c, p):
        return remote(gath.at[c, p], gath.at[c, p], right_sem.at[c, p], z_sem.at[c, p], row + 1, col)

    def left(c, p):
        return remote(gath.at[c, p], gath.at[c, p], left_sem.at[c, p], z_sem.at[c, p], row - 1, col)

    def across(c, b, p):
        return remote(gath.at[c, p], wbuf.at[b, p], across_sem.at[c, p], w_sem.at[b, p], row, c)

    def mirror():
        return remote(mir_out, mir_in, mir_sem.at[0], mir_sem.at[1], col, row)

    def dead(target, source):
        return remote(
            mir_out.at[:, :, pl.ds(0, win)], deads.at[source], dead_send.at[target],
            dead_recv.at[source], target, col,
        )

    def pair(chip, k):
        span = pl.ds(k * chunk, chunk)
        return remote(
            part_out.at[2 * chip + 1 - side, :, span], pair_in.at[chip, :, span],
            pair_send.at[chip, k], pair_recv.at[chip, k], row, mate,
        )

    def cross(chip, source, k):
        span = pl.ds(k * chunk, chunk)
        return remote(
            part_out.at[2 * chip + side, :, span], chip_in.at[source, :, span],
            chip_send.at[chip, k], chip_recv.at[source, k], row, 2 * chip + side,
        )

    def merge(chip, k):
        pair(chip, k).wait_recv()
        b = 2 * chip + side
        span = pl.ds(pl.multiple_of(k * chunk, chunk), chunk)
        part_out[b, :, span, :] = part_out[b, :, span, :] + pair_in[chip, :, span, :]
        cross(chip, home, k).start()

    owns = [
        pltpu.make_async_copy(traces.at[p, :, pl.ds(0, win)], gath.at[row, p], own_sem.at[p])
        for p in range(2)
    ]
    loads = [pltpu.make_async_copy(traces.at[p], full.at[p], full_sem.at[p]) for p in range(2)]
    for copy in owns + loads:
        copy.start()

    barrier = pltpu.get_barrier_semaphore()

    def greet(i, _):
        @pl.when(i != col)
        def _():
            pl.semaphore_signal(barrier, inc=1, device_id={"row": row, "col": i}, device_id_type=MESH)

        @pl.when(i != row)
        def _():
            pl.semaphore_signal(barrier, inc=1, device_id={"row": i, "col": col}, device_id_type=MESH)

        return 0

    lax.fori_loop(0, grid, greet, 0)

    @pl.when(row != col)
    def _():
        pl.semaphore_signal(barrier, inc=1, device_id={"row": col, "col": row}, device_id_type=MESH)
        pl.semaphore_wait(barrier, 2 * grid - 1)

    @pl.when(row == col)
    def _():
        pl.semaphore_wait(barrier, 2 * grid - 2)

    def pass_on(c, p, go_right, go_left):
        if go_right:
            @pl.when(row + 1 < grid)
            def _():
                right(c, p).start()

        if go_left:
            @pl.when(row > 0)
            def _():
                left(c, p).start()

        @pl.when(c != col)
        def _():
            across(c, col, p).start()

    for p in range(2):
        owns[p].wait()
        pass_on(row, p, True, True)

    for p in range(2):
        loads[p].wait()
        mir_out[p] = dot(hot_col[...], full[p], ((1,), (1,))).astype(BF16)

    @pl.when(row != col)
    def _():
        mirror().start()

    def send_dead(i, _):
        @pl.when(i != row)
        def _():
            dead(i, row).start()

        return 0

    lax.fori_loop(0, grid, send_dead, 0)

    def build_full():
        @pl.when(row != col)
        def _():
            mirror().wait_recv()
            mir_in[...] = mir_in[...] * patch_keep[...][None]

        @pl.when(row == col)
        def _():
            mir_in[...] = mir_out[...] * patch_keep[...][None]

        def some(k, _):
            span = pl.ds(pl.multiple_of(k * 128, 128), 128)
            for p in range(2):
                kept = full[p, span, :].astype(F32) * recv_lane[...] * live_row[span, :]
                full[p, span, :] = (kept + dot(hot_row_t[span, :], mir_in[p])).astype(BF16)
            return 0

        lax.fori_loop(0, tile // 128, some, 0)

    def widen(source, b, lost):
        for p in range(2):
            raw = source[p].astype(F32) * win_live[b] * live_col[...]
            extra = dot(hot_col_t[...], lost[p] * dead_keep[b])
            value = (raw + extra).astype(BF16)
            if p == 0:
                wide[0, :, :win] = value
                wide[1, :, win:] = value
            else:
                wide[0, :, win:] = value
                wide[1, :, :win] = -value

    def multiply():
        def block(t, _):
            chip = lax.rem(home + chips - 1 - t // 2, chips)
            mine = lax.rem(t, 2)
            b = 2 * chip + lax.rem(col + 1 + t, 2)

            @pl.when(b != row)
            def _():
                dead(b, b).wait_recv()

            @pl.when(b == row)
            def _():
                deads[row] = mir_out[:, :, :win]

            @pl.when(b != col)
            def _():
                for p in range(2):
                    across(col, b, p).wait_recv()
                widen(wbuf.at[b], b, deads.at[b])

            @pl.when(b == col)
            def _():
                widen(gath.at[col], b, deads.at[b])

            def rows(k, _):
                span = pl.ds(pl.multiple_of(k * chunk, chunk), chunk)
                both = dot(full[0, span, :], wide[0]) + dot(full[1, span, :], wide[1])
                part_out[b, 0, span, :] = both[:, :win]
                part_out[b, 1, span, :] = both[:, win:]

                @pl.when(mine == 0)
                def _():
                    pair(chip, k).start()

                @pl.when((mine == 1) & (chip != home) & inline)
                def _():
                    merge(chip, k)

                return 0

            lax.fori_loop(0, CHUNKS, rows, 0)
            return 0

        lax.fori_loop(0, grid, block, 0)

    @pl.when(far == 0)
    def _():
        build_full()

    def step(s, _):
        @pl.when(s > 0)
        def _():
            for p in range(2):
                @pl.when(row - s >= 0)
                def _():
                    left(row - s, p).wait_recv()
                    pass_on(row - s, p, True, False)

                @pl.when(row + s < grid)
                def _():
                    right(row + s, p).wait_recv()
                    pass_on(row + s, p, False, True)

        @pl.when((s == min(2, grid - 1)) & (far > 0))
        def _():
            build_full()

        @pl.when(s == turn)
        def _():
            multiply()

        @pl.when((s == last) & jnp.logical_not(inline))
        def _():
            def some(i, _):
                for k in range(CHUNKS):
                    merge(lax.rem(home + 1 + i, chips), k)
                return 0

            lax.fori_loop(0, chips - 1, some, 0)

        return 0

    lax.fori_loop(0, grid, step, 0)

    def arrive(i, _):
        for k in range(CHUNKS):
            @pl.when(i != home)
            def _():
                cross(i, i, k).wait_recv()

            @pl.when(i == home)
            def _():
                pair(home, k).wait_recv()

        return 0

    lax.fori_loop(0, chips, arrive, 0)
    first, second = wav[0] * scale, wav[1] * scale

    def finish(k, _):
        span = pl.ds(pl.multiple_of(k * 128, 128), 128)
        real = part_out[col, 0, span, :] + pair_in[home, 0, span, :]
        imag = part_out[col, 1, span, :] + pair_in[home, 1, span, :]
        for i in range(1, chips):
            other = lax.rem(home + i, chips)
            real = real + chip_in[other, 0, span, :]
            imag = imag + chip_in[other, 1, span, :]
        out[0, span, :] = full[0, span, :win].astype(F32) - (first * real - second * imag)
        out[1, span, :] = full[1, span, :win].astype(F32) - (first * imag + second * real)
        return 0

    lax.fori_loop(0, tile // 128, finish, 0)

    def drain(i, _):
        for p in range(2):
            @pl.when((row + 1 < grid) & (i <= row))
            def _():
                right(i, p).wait_send()

            @pl.when((row > 0) & (i >= row))
            def _():
                left(i, p).wait_send()

            @pl.when(i != col)
            def _():
                across(i, col, p).wait_send()

        @pl.when(i != row)
        def _():
            dead(i, row).wait_send()

        return 0

    lax.fori_loop(0, grid, drain, 0)

    def drain_sums(i, _):
        for k in range(CHUNKS):
            pair(i, k).wait_send()

            @pl.when(i != home)
            def _():
                cross(i, home, k).wait_send()

        return 0

    lax.fori_loop(0, chips, drain_sums, 0)

    @pl.when(row != col)
    def _():
        mirror().wait_send()


def make_local(order):
    def local(traces, recv_live, missing, wavelet):
        tile = traces.shape[1]
        grid = lax.axis_size("row")
        lost = missing.shape[1]
        win = 128
        row = lax.axis_index("row")
        col = lax.axis_index("col")
        positions = jnp.arange(tile, dtype=jnp.int32)
        miss_row = lax.dynamic_index_in_dim(missing, row, 0, keepdims=False)
        miss_col = lax.dynamic_index_in_dim(missing, col, 0, keepdims=False)
        hot_row = positions[None, :] == miss_row[:, None]
        hot_col = positions[None, :] == miss_col[:, None]
        live_row = ~jnp.any(hot_row, axis=0)
        live_col = ~jnp.any(hot_col, axis=0)
        dead_win = jnp.any(missing[:, :, None] == positions[None, None, :win], axis=1)
        recv = (recv_live == 1).reshape(grid, tile)
        recv_row = lax.dynamic_index_in_dim(recv, row, 0, keepdims=False)
        recv_col = lax.dynamic_index_in_dim(recv, col, 0, keepdims=False)
        recv_miss_row = jnp.any(hot_row & recv_row[None, :], axis=1)
        recv_miss_col = jnp.any(hot_col & recv_col[None, :], axis=1)
        operands = (
            wavelet,
            traces,
            hot_col.astype(BF16),
            (positions[:, None] == miss_col[None, :]).astype(BF16),
            (positions[:, None] == miss_row[None, :]).astype(BF16),
            (recv_miss_row[:, None] & live_col[None, :]).astype(BF16),
            recv_col[None, :].astype(F32),
            live_row[:, None].astype(F32),
            live_col[:, None].astype(F32),
            recv[:, None, :win].astype(F32),
            (recv_miss_col[None, :, None] & ~dead_win[:, None, :]).astype(BF16),
        )
        vmem = pl.BlockSpec(memory_space=pltpu.VMEM)
        dma = pltpu.SemaphoreType.DMA
        return pl.pallas_call(
            functools.partial(kernel, grid, 1.0 / math.sqrt(order)),
            out_shape=jax.ShapeDtypeStruct((2, tile, win), F32),
            in_specs=[pl.BlockSpec(memory_space=pltpu.SMEM), pl.BlockSpec(memory_space=pl.ANY)]
            + [vmem] * 9,
            out_specs=vmem,
            scratch_shapes=[
                pltpu.VMEM((2, tile, tile), BF16),
                pltpu.VMEM((grid, 2, tile, win), BF16),
                pltpu.VMEM((grid, 2, tile, win), BF16),
                pltpu.VMEM((2, lost, tile), BF16),
                pltpu.VMEM((2, lost, tile), BF16),
                pltpu.VMEM((grid, 2, lost, win), BF16),
                pltpu.VMEM((2, tile, 2 * win), BF16),
                pltpu.VMEM((grid, 2, tile, win), F32),
                pltpu.VMEM((grid // 2, 2, tile, win), F32),
                pltpu.VMEM((grid // 2, 2, tile, win), F32),
                dma((2,)), dma((2,)), dma((grid, 2)), dma((grid, 2)), dma((grid, 2)),
                dma((grid, 2)), dma((grid, 2)), dma((2,)), dma((grid,)), dma((grid,)),
                dma((grid // 2, CHUNKS)), dma((grid // 2, CHUNKS)),
                dma((grid // 2, CHUNKS)), dma((grid // 2, CHUNKS)),
            ],
            compiler_params=pltpu.CompilerParams(
                collective_id=0, has_side_effects=True, vmem_limit_bytes=60 * 1024 * 1024
            ),
            name="predict",
        )(*operands)

    return local


def solution(mesh):
    in_specs = (P("freq", "row", "col"), P("freq"), P("freq", None), P("freq"))
    out_specs = P("freq", "row", "col")

    def run(traces, recv_live, missing, wavelet):
        local = make_local(traces.shape[1])
        return jax.shard_map(
            local, mesh=mesh, in_specs=in_specs, out_specs=out_specs, check_vma=False
        )(traces, recv_live, missing, wavelet)

    return run
```
